32 devices in a mesh: groups: 2 (over y), tm: 4 (over x, core), win: 4 (over z).
Axes of the slice: x: 2, y: 2, z: 4, core: 2. Of those that a mesh axis runs over, the one named last changes fastest.
Arguments:
- unitaries: float32 [8, 4, 2, 2, 256, 256], P(('groups', 'win'), 'tm'), parts along dimension 0, may hold values from -1 to 1, as said below
Outputs:
- propagators: float32 [8, 4, 2, 2, 256, 256], P(('groups', 'win'), 'tm'), parts along dimension 0
The draws below stay inside these ranges and needn't reach their ends.
There are 2 independent parts, one for each index of `groups`. The reference program is written for one: setup_inputs(seed, part) draws one part's arguments, and reference() takes and returns one part's arrays. A program takes and returns all parts, laid end to end along the dimension named above; each array names one. Nothing has to cross between parts.
Inputs may be any that keep to these rules, and one draw needn't show every extreme that they name: `unitaries`: each slot's complex matrix is unitary.
All inputs are finite; a program needn't handle non-finite values.
Results may differ from the reference program's by a relative error of at most 0.0003.
Values sent between devices are 32-bit elements; how exact they have to be, the bound alone decides.
A program may use at most 64 MiB of HBM per device.

```python
import math
import jax
import jax.numpy as jnp
from jax import lax

DIM = 256
SLOTS = 2
WIN_DEVS = 4
WINDOWS = 4


def draw_unitaries(key, part):
    slot_count = WINDOWS * WIN_DEVS * SLOTS
    qubits = DIM.bit_length() - 1
    subkeys = jax.random.split(key, 3)

    def rotations(rkey):
        akey, bkey, ckey = jax.random.split(rkey, 3)
        tilt_angle = jax.random.uniform(akey, (slot_count, qubits), jnp.float32, 0.25, 1.3)
        phase_one = jax.random.uniform(bkey, (slot_count, qubits), jnp.float32, -math.pi, math.pi)
        phase_two = jax.random.uniform(ckey, (slot_count, qubits), jnp.float32, -math.pi, math.pi)
        cosine = jnp.cos(tilt_angle)
        sine = jnp.sin(tilt_angle)
        top_real = jnp.stack([cosine * jnp.cos(phase_one), -sine * jnp.cos(phase_two)], axis=-1)
        low_real = jnp.stack([sine * jnp.cos(phase_two), cosine * jnp.cos(phase_one)], axis=-1)
        top_imag = jnp.stack([cosine * jnp.sin(phase_one), sine * jnp.sin(phase_two)], axis=-1)
        low_imag = jnp.stack([sine * jnp.sin(phase_two), -cosine * jnp.sin(phase_one)], axis=-1)
        return (jnp.stack([top_real, low_real], axis=-2), jnp.stack([top_imag, low_imag], axis=-2))
    first_real, first_imag = rotations(subkeys[0])
    kron_real = jnp.ones((slot_count, 1, 1), jnp.float32)
    kron_imag = jnp.zeros((slot_count, 1, 1), jnp.float32)
    for q in range(qubits):
        gate_real = first_real[:, q]
        gate_imag = first_imag[:, q]
        size_now = kron_real.shape[1] * 2
        new_real = kron_real[:, :, None, :, None] * gate_real[:, None, :, None, :] - kron_imag[:, :, None, :, None] * gate_imag[:, None, :, None, :]
        new_imag = kron_real[:, :, None, :, None] * gate_imag[:, None, :, None, :] + kron_imag[:, :, None, :, None] * gate_real[:, None, :, None, :]
        kron_real = new_real.reshape((slot_count, size_now, size_now))
        kron_imag = new_imag.reshape((slot_count, size_now, size_now))
    phases = jax.random.uniform(subkeys[1], (slot_count, DIM, 1), jnp.float32, -math.pi, math.pi)
    mixed_real = jnp.cos(phases) * kron_real - jnp.sin(phases) * kron_imag
    mixed_imag = jnp.cos(phases) * kron_imag + jnp.sin(phases) * kron_real
    second_real, second_imag = rotations(subkeys[2])
    for q in range(qubits):
        gate_real = second_real[:, q]
        gate_imag = second_imag[:, q]
        shaped = (slot_count, 2 ** q, 2, 2 ** (qubits - 1 - q), DIM)
        block_real = mixed_real.reshape(shaped)
        block_imag = mixed_imag.reshape(shaped)
        new_real = jnp.einsum('nij,najbc->naibc', gate_real, block_real) - jnp.einsum('nij,najbc->naibc', gate_imag, block_imag)
        new_imag = jnp.einsum('nij,najbc->naibc', gate_real, block_imag) + jnp.einsum('nij,najbc->naibc', gate_imag, block_real)
        mixed_real = new_real.reshape((slot_count, DIM, DIM))
        mixed_imag = new_imag.reshape((slot_count, DIM, DIM))
    stacked = jnp.stack([mixed_real, mixed_imag], axis=1)
    return stacked.reshape((WINDOWS, WIN_DEVS, SLOTS, 2, DIM, DIM)).astype(jnp.float32)


def setup_inputs(seed: int = 0, part: int = 0) -> dict:
    arg_keys = jax.random.split(jax.random.key(seed), 2)
    part_splits = jax.random.split(jax.random.fold_in(arg_keys[1], part), 2)
    unitaries = draw_unitaries(jax.random.fold_in(jax.random.fold_in(arg_keys[1], part), 71), part)
    return {"unitaries": unitaries}


def complex_product(left, right):
    hi = lax.Precision.HIGHEST
    real_part = jnp.dot(left[0], right[0], precision=hi, preferred_element_type=jnp.float32) - jnp.dot(left[1], right[1], precision=hi, preferred_element_type=jnp.float32)
    imag_part = jnp.dot(left[0], right[1], precision=hi, preferred_element_type=jnp.float32) + jnp.dot(left[1], right[0], precision=hi, preferred_element_type=jnp.float32)
    return jnp.stack([real_part, imag_part])


def reference(unitaries):
    shape = unitaries.shape
    width = shape[-1]
    sequence = unitaries.reshape((-1, 2, width, width))
    start = jnp.stack([jnp.eye(width, dtype=jnp.float32), jnp.zeros((width, width), jnp.float32)])

    def advance(running, factor):
        updated = complex_product(factor, running)
        return updated, updated

    final_value, history = lax.scan(advance, start, sequence)
    return history.reshape(shape)
```

```python
import functools
import jax
import jax.numpy as jnp
from jax import lax
from jax.sharding import PartitionSpec as P
from jax.experimental import pallas as pl
from jax.experimental.pallas import tpu as pltpu

F32 = jnp.float32
BF16 = jnp.bfloat16
MESH = pl.DeviceIdType.MESH
CHUNKS = 2


def split(a):
    hi = a.astype(BF16)
    return hi, (a - hi.astype(F32)).astype(BF16)


def real_dot(a, b, dims):
    def dot(p, q):
        return lax.dot_general(p, q, (dims, ((), ())), preferred_element_type=F32)

    return dot(a[0], b[0]) + (dot(a[0], b[1]) + dot(a[1], b[0]))


def product(a, b, transposed=False):
    dims = ((1,), (1,)) if transposed else ((1,), (0,))
    ar, ai = split(a[0]), split(a[1])
    br, bi = split(b[0]), split(b[1])
    real = real_dot(ar, br, dims) - real_dot(ai, bi, dims)
    imag = real_dot(ar, bi, dims) + real_dot(ai, br, dims)
    return real, imag


def pair(ref):
    return ref[0], ref[1]


def put(ref, value):
    ref[0] = value[0]
    ref[1] = value[1]


def kernel(
    tm, windows, u, out,
    total, sib, chips, win, first, second, carry, nxt,
    t_send, t_recv, c_send, c_recv, f_send, f_recv,
    z_send, z_recv, e_send, e_recv, g_send, g_recv,
):
    d = lax.axis_index("tm")
    z = lax.axis_index("win")
    x, c = d // 2, d % 2
    nx = tm // 2
    width = u.shape[-1]
    half = width // 2
    rows = width // tm
    step = rows // CHUNKS
    mate = {"tm": x * 2 + (1 - c)}

    barrier = pltpu.get_barrier_semaphore()

    def greet(to):
        pl.semaphore_signal(barrier, inc=1, device_id=to, device_id_type=MESH)

    greet(mate)
    for o in range(1, nx):
        greet({"tm": ((x + o) % nx) * 2 + c})

    @pl.when(z > 0)
    def _():
        greet({"win": z - 1})

    @pl.when(z < windows - 1)
    def _():
        greet({"win": z + 1})

    put(total, product(pair(u.at[1]), pair(u.at[0])))
    inner = (z > 0) & (z < windows - 1)

    @pl.when(inner)
    def _():
        pl.semaphore_wait(barrier, nx + 2)

    @pl.when(jnp.logical_not(inner))
    def _():
        pl.semaphore_wait(barrier, nx + 1)

    def copy(src, dst, send, recv, to):
        return pltpu.make_async_remote_copy(
            src_ref=src, dst_ref=dst, send_sem=send, recv_sem=recv,
            device_id=to, device_id_type=MESH,
        )

    t_copy = copy(total, sib, t_send, t_recv, mate)
    t_copy.start()
    t_copy.wait_recv()

    @pl.when(c == 0)
    def _():
        put(chips.at[x], product(pair(sib), pair(total)))

    @pl.when(c == 1)
    def _():
        put(chips.at[x], product(pair(total), pair(sib)))

    own_half = pl.ds(pl.multiple_of(c * half, half), half)
    other_half = pl.ds(pl.multiple_of((1 - c) * half, half), half)

    def c_copy(j, to):
        ref = chips.at[j, :, own_half, :]
        return copy(ref, ref, c_send.at[to], c_recv.at[j], {"tm": to * 2 + c})

    def f_copy(j, part):
        ref = chips.at[j, :, part, :]
        return copy(ref, ref, f_send.at[j], f_recv.at[j], mate)

    others = [(x + o) % nx for o in range(1, nx)]
    for j in others:
        c_copy(x, j).start()

    @pl.when(c == 0)
    def _():
        put(first, pair(u.at[0]))
        put(second, pair(total))

    @pl.when(c == 1)
    def _():
        put(first, product(pair(u.at[0]), pair(sib)))
        put(second, pair(chips.at[x]))

    for j in others:
        c_copy(j, x).wait_recv()
        f_copy(j, own_half).start()
    for j in others:
        f_copy(j, other_half).wait_recv()

    put(win, pair(chips.at[0]))

    def apply_before():
        before = pair(win)
        put(first, product(pair(first), before))
        put(second, product(pair(second), before))

    def join(j, _):
        @pl.when((j == x) & (z > 0))
        def _():
            apply_before()

        put(win, product(pair(chips.at[j]), pair(win)))
        return 0

    if nx == 2:
        @pl.when((x == 1) & (z > 0))
        def _():
            apply_before()

        put(win, product(pair(chips.at[1]), pair(win)))
    else:
        lax.fori_loop(1, nx, join, 0)

    def piece(owner, k):
        return pl.ds(pl.multiple_of(owner * rows + k * step, step), step)

    def z_copy(k):
        return copy(
            nxt.at[k], carry.at[:, piece(d, k), :], z_send.at[k], z_recv.at[k], {"win": z + 1}
        )

    def advance(k, held):
        put(nxt.at[k], product(held, pair(win), transposed=True))
        z_copy(k).start()

    def e_copy(j, to, k):
        ref = carry.at[:, piece(j * 2 + c, k), :]
        return copy(ref, ref, e_send.at[to, k], e_recv.at[j, k], {"tm": to * 2 + c})

    def g_copy(j, core, k):
        ref = carry.at[:, piece(j * 2 + core, k), :]
        return copy(ref, ref, g_send.at[j, k], g_recv.at[j, k], mate)

    @pl.when(z == 0)
    def _():
        for k in range(CHUNKS):
            row = lax.broadcasted_iota(jnp.int32, (step, width), 0) + (d * rows + k * step)
            column = lax.broadcasted_iota(jnp.int32, (step, width), 1)
            advance(k, ((row == column).astype(F32), jnp.zeros((step, width), F32)))

        if nx > 2:
            put(win, pair(chips.at[0]))

            def redo(j, _):
                @pl.when(j == x)
                def _():
                    apply_before()

                put(win, product(pair(chips.at[j]), pair(win)))
                return 0

            lax.fori_loop(1, nx, redo, 0)
        else:
            put(win, pair(chips.at[0]))

            @pl.when(x == 1)
            def _():
                apply_before()

        put(out.at[0], pair(first))
        put(out.at[1], pair(second))

    @pl.when(z > 0)
    def _():
        for k in range(CHUNKS):
            ref = carry.at[:, piece(d, k), :]
            copy(nxt.at[k], ref, z_send.at[k], z_recv.at[k], {"win": z - 1}).wait_recv()
            for j in others:
                e_copy(x, j, k).start()
            g_copy(x, c, k).start()

            @pl.when(z < windows - 1)
            def _():
                advance(k, pair(ref))

        for k in range(CHUNKS):
            for j in others:
                e_copy(j, x, k).wait_recv()
                g_copy(j, c, k).start()
        for k in range(CHUNKS):
            g_copy(x, 1 - c, k).wait_recv()
            for j in others:
                g_copy(j, 1 - c, k).wait_recv()
        before = pair(carry)
        put(out.at[0], product(pair(first), before, transposed=True))
        put(out.at[1], product(pair(second), before, transposed=True))
        for k in range(CHUNKS):
            for j in others:
                e_copy(x, j, k).wait_send()
                g_copy(j, c, k).wait_send()
            g_copy(x, c, k).wait_send()

    @pl.when(z < windows - 1)
    def _():
        for k in range(CHUNKS):
            z_copy(k).wait_send()

    t_copy.wait_send()
    for j in others:
        c_copy(x, j).wait_send()
        f_copy(j, own_half).wait_send()


def on_device(tm, windows, unitaries):
    u = unitaries[0, 0]
    width = u.shape[-1]
    nx = tm // 2
    dma = pltpu.SemaphoreType.DMA
    mat = pltpu.VMEM((2, width, width), F32)
    step = width // tm // CHUNKS
    result = pl.pallas_call(
        functools.partial(kernel, tm, windows),
        out_shape=jax.ShapeDtypeStruct(u.shape, F32),
        in_specs=[pl.BlockSpec(memory_space=pltpu.VMEM)],
        out_specs=pl.BlockSpec(memory_space=pltpu.VMEM),
        scratch_shapes=[
            mat, mat, pltpu.VMEM((nx, 2, width, width), F32), mat, mat, mat, mat,
            pltpu.VMEM((CHUNKS, 2, step, width), F32),
            dma, dma, dma((nx,)), dma((nx,)), dma((nx,)), dma((nx,)),
            dma((CHUNKS,)), dma((CHUNKS,)),
            dma((nx, CHUNKS)), dma((nx, CHUNKS)), dma((nx, CHUNKS)), dma((nx, CHUNKS)),
        ],
        compiler_params=pltpu.CompilerParams(
            collective_id=0, has_side_effects=True, vmem_limit_bytes=40 * 1024 * 1024
        ),
    )(u)
    return result[None, None]


def solution(mesh):
    placed = P(("groups", "win"), "tm", None, None, None, None)
    return jax.shard_map(
        functools.partial(on_device, mesh.shape["tm"], mesh.shape["win"]),
        mesh=mesh,
        in_specs=(placed,),
        out_specs=placed,
        check_vma=False,
    )
```

```python
import functools
import jax
import jax.numpy as jnp
from jax import lax
from jax.sharding import PartitionSpec as P
from jax.experimental import pallas as pl
from jax.experimental.pallas import tpu as pltpu

F32 = jnp.float32
BF16 = jnp.bfloat16
MESH = pl.DeviceIdType.MESH
CHUNKS = 2
PIECES = 2
NT = (((1,), (1,)), ((), ()))
NN = (((1,), (0,)), ((), ()))


def split(a):
    hi = a.astype(BF16)
    return hi, (a - hi.astype(F32)).astype(BF16)


def real_dot(a, b, dims):
    def dot(p, q):
        return lax.dot_general(p, q, dims, preferred_element_type=F32)

    return dot(a[0], b[0]) + (dot(a[0], b[1]) + dot(a[1], b[0]))


def product(a, b, transposed=False):
    dims = NT if transposed else NN
    ar, ai = split(a[0]), split(a[1])
    br, bi = split(b[0]), split(b[1])
    real = real_dot(ar, br, dims) - real_dot(ai, bi, dims)
    imag = real_dot(ar, bi, dims) + real_dot(ai, br, dims)
    return real, imag


def put_split(ref, value):
    ref[0], ref[1] = split(value[0])
    ref[2], ref[3] = split(value[1])


def row_product(a, w):
    m = a[0].shape[0]
    (rh, rl), (ih, il) = split(a[0]), split(a[1])
    stack = jnp.concatenate([rh, ih, rl, il], axis=0)
    top = jnp.concatenate([rh, ih], axis=0)

    def dot(p, q):
        return lax.dot_general(p, q, NT, preferred_element_type=F32)

    by_real = dot(stack, w[0])
    by_real = by_real[: 2 * m] + by_real[2 * m :] + dot(top, w[1])
    by_imag = dot(stack, w[2])
    by_imag = by_imag[: 2 * m] + by_imag[2 * m :] + dot(top, w[3])
    return by_real[:m] - by_imag[m:], by_real[m:] + by_imag[:m]


def pair(ref):
    return ref[0], ref[1]


def put(ref, value):
    ref[0] = value[0]
    ref[1] = value[1]


def kernel(
    tm, windows, u_hbm, out,
    u, total, sib, chips, win, first, second, carry, nxt, wsp,
    u_sem, t_send, t_recv, c_send, c_recv, f_send, f_recv,
    s_send, s_recv, z_send, z_recv, e_send, e_recv, g_send, g_recv,
):
    d = lax.axis_index("tm")
    z = lax.axis_index("win")
    x, c = d // 2, d % 2
    nx = tm // 2
    direct = nx == 2
    width = u.shape[-1]
    half = width // 2
    rows = width // tm
    step = rows // CHUNKS
    part = half // PIECES
    mate = {"tm": x * 2 + (1 - c)}
    last = windows - 1

    loads = [pltpu.make_async_copy(u_hbm.at[s], u.at[s], u_sem.at[s]) for s in range(2)]
    for load in loads:
        load.start()

    barrier = pltpu.get_barrier_semaphore()

    def greet(to):
        pl.semaphore_signal(barrier, inc=1, device_id=to, device_id_type=MESH)

    greet(mate)
    for o in range(1, nx):
        greet({"tm": ((x + o) % nx) * 2 + c})

    if direct:
        @pl.when(z > 1)
        def _():
            greet({"win": z - 1})

        @pl.when(z == 1)
        def _():
            greet({"win": 0, "tm": 2 + c})

        @pl.when((z == 0) & (x == 1))
        def _():
            greet({"win": 1, "tm": c})
            greet({"win": 1, "tm": 2 + c})

        @pl.when((z > 0) & (z < last))
        def _():
            greet({"win": z + 1})
    else:
        @pl.when(z > 0)
        def _():
            greet({"win": z - 1})

        @pl.when(z < last)
        def _():
            greet({"win": z + 1})

    for load in loads:
        load.wait()
    put(total, product(pair(u.at[1]), pair(u.at[0])))

    inner = (z > 0) & (z < last)
    if direct:
        start = (z == 0) & (x == 0)
        many = inner | ((z == 0) & (x == 1))

        @pl.when(start)
        def _():
            pl.semaphore_wait(barrier, nx)

        @pl.when(many)
        def _():
            pl.semaphore_wait(barrier, nx + 2)

        @pl.when(z == last)
        def _():
            pl.semaphore_wait(barrier, nx + 1)
    else:
        @pl.when(inner)
        def _():
            pl.semaphore_wait(barrier, nx + 2)

        @pl.when(jnp.logical_not(inner))
        def _():
            pl.semaphore_wait(barrier, nx + 1)

    def copy(src, dst, send, recv, to):
        return pltpu.make_async_remote_copy(
            src_ref=src, dst_ref=dst, send_sem=send, recv_sem=recv,
            device_id=to, device_id_type=MESH,
        )

    t_copy = copy(total, sib, t_send, t_recv, mate)
    t_copy.start()
    t_copy.wait_recv()

    @pl.when(c == 0)
    def _():
        put(chips.at[x], product(pair(sib), pair(total)))

    @pl.when(c == 1)
    def _():
        put(chips.at[x], product(pair(total), pair(sib)))

    others = [(x + o) % nx for o in range(1, nx)]

    def local():
        @pl.when(c == 0)
        def _():
            put(first, pair(u.at[0]))
            put(second, pair(total))

        @pl.when(c == 1)
        def _():
            put(first, product(pair(u.at[0]), pair(sib)))
            put(second, pair(chips.at[x]))

    def band(core, q):
        return pl.ds(pl.multiple_of(core * half + q * part, part), part)

    def c_copy(j, to, q):
        ref = chips.at[j, :, band(c, q), :]
        return copy(ref, ref, c_send.at[to, q], c_recv.at[j, q], {"tm": to * 2 + c})

    def f_copy(j, core, q):
        ref = chips.at[j, :, band(core, q), :]
        return copy(ref, ref, f_send.at[j, q], f_recv.at[j, q], mate)

    def exchange():
        for q in range(PIECES):
            for j in others:
                c_copy(x, j, q).start()
        local()
        for q in range(PIECES):
            for j in others:
                c_copy(j, x, q).wait_recv()
                f_copy(j, c, q).start()
        for q in range(PIECES):
            for j in others:
                f_copy(j, 1 - c, q).wait_recv()

    def exchange_sent():
        for q in range(PIECES):
            for j in others:
                c_copy(x, j, q).wait_send()
                f_copy(j, c, q).wait_send()

    def apply_before(before):
        put(first, product(pair(first), before))
        put(second, product(pair(second), before))

    def whole_window():
        if direct:
            put(win, product(pair(chips.at[1]), pair(chips.at[0])))
        else:
            put(win, pair(chips.at[0]))

            def join(j, _):
                put(win, product(pair(chips.at[j]), pair(win)))
                return 0

            lax.fori_loop(1, nx, join, 0)
        put_split(wsp, pair(win))

    def chips_before():
        @pl.when(x > 0)
        def _():
            if not direct:
                put(win, pair(chips.at[0]))

                def join(j, _):
                    put(win, product(pair(chips.at[j]), pair(win)))
                    return 0

                lax.fori_loop(1, x, join, 0)
                apply_before(pair(win))
            else:
                apply_before(pair(chips.at[0]))

    def piece(owner, k):
        return pl.ds(pl.multiple_of(owner * rows + k * step, step), step)

    def identity_rows(owner, k):
        row = lax.broadcasted_iota(jnp.int32, (step, width), 0) + (owner * rows + k * step)
        column = lax.broadcasted_iota(jnp.int32, (step, width), 1)
        return (row == column).astype(F32)

    def z_copy(k, to):
        return copy(
            nxt.at[k, :, pl.ds(0, step), :], carry.at[:, piece(d, k), :],
            z_send.at[k, 0], z_recv.at[k], {"win": to},
        )

    def e_copy(j, to, k):
        ref = carry.at[:, piece(j * 2 + c, k), :]
        return copy(ref, ref, e_send.at[to, k], e_recv.at[j, k], {"tm": to * 2 + c})

    def g_copy(j, core, k):
        ref = carry.at[:, piece(j * 2 + core, k), :]
        return copy(ref, ref, g_send.at[j, k], g_recv.at[j, k], mate)

    def finish():
        before = pair(carry)
        put(out.at[0], product(pair(first), before, transposed=True))
        put(out.at[1], product(pair(second), before, transposed=True))

    def finish_first():
        put(out.at[0], pair(first))
        put(out.at[1], pair(second))

    if direct:
        def s_copy(k, i):
            return copy(
                nxt.at[k, :, pl.ds(i * step, step), :], carry.at[:, piece(2 * i + c, k), :],
                s_send.at[k, i], s_recv.at[k, i], {"tm": 2 + c},
            )

        def o_copy(k, i):
            return copy(
                nxt.at[k, :, pl.ds(i * step, step), :], carry.at[:, piece(2 * i + c, k), :],
                z_send.at[k, i], z_recv.at[k], {"win": 1, "tm": 2 * i + c},
            )

        @pl.when((z == 0) & (x == 0))
        def _():
            put_split(wsp, pair(chips.at[0]))
            for k in range(CHUNKS):
                real = jnp.concatenate([identity_rows(c, k), identity_rows(2 + c, k)], axis=0)
                put(nxt.at[k], row_product((real, jnp.zeros_like(real)), wsp))
                for i in range(2):
                    s_copy(k, i).start()
            local()
            finish_first()
            for k in range(CHUNKS):
                for i in range(2):
                    s_copy(k, i).wait_send()

        @pl.when((z == 0) & (x == 1))
        def _():
            put_split(wsp, pair(chips.at[1]))
            for k in range(CHUNKS):
                for i in range(2):
                    s_copy(k, i).wait_recv()
                    g_copy(i, c, k).start()
                held = [
                    jnp.concatenate([carry[p, piece(c, k), :], carry[p, piece(2 + c, k), :]], axis=0)
                    for p in range(2)
                ]
                put(nxt.at[k], row_product(held, wsp))
                for i in range(2):
                    o_copy(k, i).start()
            local()
            for k in range(CHUNKS):
                for i in range(2):
                    g_copy(i, 1 - c, k).wait_recv()
            finish()
            for k in range(CHUNKS):
                for i in range(2):
                    g_copy(i, c, k).wait_send()
                    o_copy(k, i).wait_send()
    else:
        @pl.when(z == 0)
        def _():
            exchange()
            whole_window()
            for k in range(CHUNKS):
                real = identity_rows(d, k)
                put(nxt.at[k, :, pl.ds(0, step), :], row_product((real, jnp.zeros_like(real)), wsp))
                z_copy(k, 1).start()
            chips_before()
            finish_first()
            for k in range(CHUNKS):
                z_copy(k, 1).wait_send()
            exchange_sent()

    @pl.when(z > 0)
    def _():
        exchange()

        @pl.when(z < last)
        def _():
            whole_window()

        @pl.when(z > 1)
        def _():
            chips_before()

        for k in range(CHUNKS):
            ref = carry.at[:, piece(d, k), :]
            z_copy(k, z).wait_recv()
            for j in others:
                e_copy(x, j, k).start()
            g_copy(x, c, k).start()

            @pl.when(z < last)
            def _():
                put(nxt.at[k, :, pl.ds(0, step), :], row_product(pair(ref), wsp))
                z_copy(k, z + 1).start()

        for k in range(CHUNKS):
            for j in others:
                e_copy(j, x, k).wait_recv()
                g_copy(j, c, k).start()

        @pl.when(z == 1)
        def _():
            chips_before()

        for k in range(CHUNKS):
            g_copy(x, 1 - c, k).wait_recv()
            for j in others:
                g_copy(j, 1 - c, k).wait_recv()
        finish()
        for k in range(CHUNKS):
            for j in others:
                e_copy(x, j, k).wait_send()
                g_copy(j, c, k).wait_send()
            g_copy(x, c, k).wait_send()

        @pl.when(z < last)
        def _():
            for k in range(CHUNKS):
                z_copy(k, z + 1).wait_send()

        exchange_sent()

    t_copy.wait_send()


def on_device(tm, windows, unitaries):
    u = unitaries[0, 0]
    width = u.shape[-1]
    nx = tm // 2
    dma = pltpu.SemaphoreType.DMA
    mat = pltpu.VMEM((2, width, width), F32)
    step = width // tm // CHUNKS
    result = pl.pallas_call(
        functools.partial(kernel, tm, windows),
        out_shape=jax.ShapeDtypeStruct(u.shape, F32),
        in_specs=[pl.BlockSpec(memory_space=pl.ANY)],
        out_specs=pl.BlockSpec(memory_space=pltpu.VMEM),
        scratch_shapes=[
            pltpu.VMEM((2, 2, width, width), F32),
            mat, mat, pltpu.VMEM((nx, 2, width, width), F32), mat, mat, mat, mat,
            pltpu.VMEM((CHUNKS, 2, 2 * step, width), F32),
            pltpu.VMEM((4, width, width), BF16),
            dma((2,)), dma, dma,
            dma((nx, PIECES)), dma((nx, PIECES)), dma((nx, PIECES)), dma((nx, PIECES)),
            dma((CHUNKS, 2)), dma((CHUNKS, 2)), dma((CHUNKS, 2)), dma((CHUNKS,)),
            dma((nx, CHUNKS)), dma((nx, CHUNKS)), dma((nx, CHUNKS)), dma((nx, CHUNKS)),
        ],
        compiler_params=pltpu.CompilerParams(
            collective_id=0, has_side_effects=True, vmem_limit_bytes=40 * 1024 * 1024
        ),
    )(u)
    return result[None, None]


def solution(mesh):
    placed = P(("groups", "win"), "tm", None, None, None, None)
    return jax.shard_map(
        functools.partial(on_device, mesh.shape["tm"], mesh.shape["win"]),
        mesh=mesh,
        in_specs=(placed,),
        out_specs=placed,
        check_vma=False,
    )
```

```python
import functools
import jax
import jax.numpy as jnp
from jax import lax
from jax.sharding import PartitionSpec as P
from jax.experimental import pallas as pl
from jax.experimental.pallas import tpu as pltpu

F32 = jnp.float32
BF16 = jnp.bfloat16
MESH = pl.DeviceIdType.MESH
MOST_CHUNKS = 4
LEAD = 4
PIECES = 2
NT = (((1,), (1,)), ((), ()))
NN = (((1,), (0,)), ((), ()))


def split(a):
    hi = a.astype(BF16)
    return hi, (a - hi.astype(F32)).astype(BF16)


def real_dot(a, b, dims):
    def dot(p, q):
        return lax.dot_general(p, q, dims, preferred_element_type=F32)

    return dot(a[0], b[0]) + (dot(a[0], b[1]) + dot(a[1], b[0]))


def product(a, b, transposed=False):
    dims = NT if transposed else NN
    ar, ai = split(a[0]), split(a[1])
    br, bi = split(b[0]), split(b[1])
    real = real_dot(ar, br, dims) - real_dot(ai, bi, dims)
    imag = real_dot(ar, bi, dims) + real_dot(ai, br, dims)
    return real, imag


def put_split(ref, value):
    ref[0], ref[1] = split(value[0])
    ref[2], ref[3] = split(value[1])


def row_product(a, w):
    m = a[0].shape[0]
    (rh, rl), (ih, il) = split(a[0]), split(a[1])
    stack = jnp.concatenate([rh, ih, rl, il], axis=0)
    top = jnp.concatenate([rh, ih], axis=0)

    def dot(p, q):
        return lax.dot_general(p, q, NT, preferred_element_type=F32)

    by_real = dot(stack, w[0])
    by_real = by_real[: 2 * m] + by_real[2 * m :] + dot(top, w[1])
    by_imag = dot(stack, w[2])
    by_imag = by_imag[: 2 * m] + by_imag[2 * m :] + dot(top, w[3])
    return by_real[:m] - by_imag[m:], by_real[m:] + by_imag[:m]


def pair(ref):
    return ref[0], ref[1]


def put(ref, value):
    ref[0] = value[0]
    ref[1] = value[1]


def carry_chunks(rows):
    return max(1, min(MOST_CHUNKS, rows // 8))


def kernel(
    tm, windows, u_hbm, out,
    u, total, sib, chips, win, first, second, carry, nxt, wsp,
    u_sem, t_send, t_recv, c_send, c_recv, f_send, f_recv,
    s_send, s_recv, z_send, z_recv, e_send, e_recv, g_send, g_recv,
):
    d = lax.axis_index("tm")
    z = lax.axis_index("win")
    x, c = d // 2, d % 2
    nx = tm // 2
    direct = nx == 2
    width = u.shape[-1]
    half = width // 2
    rows = width // tm
    chunks = carry_chunks(rows)
    step = rows // chunks
    part = half // PIECES
    mate = {"tm": x * 2 + (1 - c)}
    last = windows - 1

    loads = [pltpu.make_async_copy(u_hbm.at[s], u.at[s], u_sem.at[s]) for s in range(2)]
    for load in loads:
        load.start()

    barrier = pltpu.get_barrier_semaphore()

    def greet(to):
        pl.semaphore_signal(barrier, inc=1, device_id=to, device_id_type=MESH)

    greet(mate)
    for o in range(1, nx):
        greet({"tm": ((x + o) % nx) * 2 + c})

    @pl.when(z > 0)
    def _():
        greet({"win": z - 1})

    @pl.when(z < last)
    def _():
        greet({"win": z + 1})

    for load in loads:
        load.wait()
    put(total, product(pair(u.at[1]), pair(u.at[0])))

    inner = (z > 0) & (z < last)
    @pl.when(inner)
    def _():
        pl.semaphore_wait(barrier, nx + 2)

    @pl.when(jnp.logical_not(inner))
    def _():
        pl.semaphore_wait(barrier, nx + 1)

    def copy(src, dst, send, recv, to):
        return pltpu.make_async_remote_copy(
            src_ref=src, dst_ref=dst, send_sem=send, recv_sem=recv,
            device_id=to, device_id_type=MESH,
        )

    t_copy = copy(total, sib, t_send, t_recv, mate)
    t_copy.start()
    t_copy.wait_recv()

    @pl.when(c == 0)
    def _():
        put(chips.at[x], product(pair(sib), pair(total)))

    @pl.when(c == 1)
    def _():
        put(chips.at[x], product(pair(total), pair(sib)))

    others = [(x + o) % nx for o in range(1, nx)]

    def local():
        @pl.when(c == 0)
        def _():
            put(first, pair(u.at[0]))
            put(second, pair(total))

        @pl.when(c == 1)
        def _():
            put(first, product(pair(u.at[0]), pair(sib)))
            put(second, pair(chips.at[x]))

    def band(core, q):
        return pl.ds(pl.multiple_of(core * half + q * part, part), part)

    def c_copy(j, to, q):
        ref = chips.at[j, :, band(c, q), :]
        return copy(ref, ref, c_send.at[to, q], c_recv.at[j, q], {"tm": to * 2 + c})

    def f_copy(j, core, q):
        ref = chips.at[j, :, band(core, q), :]
        return copy(ref, ref, f_send.at[j, q], f_recv.at[j, q], mate)

    def exchange():
        for q in range(PIECES):
            for j in others:
                c_copy(x, j, q).start()
        local()
        for q in range(PIECES):
            for j in others:
                c_copy(j, x, q).wait_recv()
                f_copy(j, c, q).start()
        for q in range(PIECES):
            for j in others:
                f_copy(j, 1 - c, q).wait_recv()

    def exchange_sent():
        for q in range(PIECES):
            for j in others:
                c_copy(x, j, q).wait_send()
                f_copy(j, c, q).wait_send()

    def apply_before(before):
        put(first, product(pair(first), before))
        put(second, product(pair(second), before))

    def whole_window():
        if direct:
            put(win, product(pair(chips.at[1]), pair(chips.at[0])))
        else:
            put(win, pair(chips.at[0]))

            def join(j, _):
                put(win, product(pair(chips.at[j]), pair(win)))
                return 0

            lax.fori_loop(1, nx, join, 0)
        put_split(wsp, pair(win))

    def chips_before():
        @pl.when(x > 0)
        def _():
            if not direct:
                put(win, pair(chips.at[0]))

                def join(j, _):
                    put(win, product(pair(chips.at[j]), pair(win)))
                    return 0

                lax.fori_loop(1, x, join, 0)
                apply_before(pair(win))
            else:
                apply_before(pair(chips.at[0]))

    def piece(owner, k):
        return pl.ds(pl.multiple_of(owner * rows + k * step, step), step)

    def identity_rows(owner, k):
        row = lax.broadcasted_iota(jnp.int32, (step, width), 0) + (owner * rows + k * step)
        column = lax.broadcasted_iota(jnp.int32, (step, width), 1)
        return (row == column).astype(F32)

    def z_copy(k, to):
        return copy(
            nxt.at[k, 0], carry.at[:, piece(d, k), :],
            z_send.at[k, 0], z_recv.at[k], {"win": to},
        )

    def e_copy(j, to, k):
        ref = carry.at[:, piece(j * 2 + c, k), :]
        return copy(ref, ref, e_send.at[to, k], e_recv.at[j, k], {"tm": to * 2 + c})

    def g_copy(j, core, k):
        ref = carry.at[:, piece(j * 2 + core, k), :]
        return copy(ref, ref, g_send.at[j, k], g_recv.at[j, k], mate)

    def finish():
        before = pair(carry)
        put(out.at[0], product(pair(first), before, transposed=True))
        put(out.at[1], product(pair(second), before, transposed=True))

    def finish_first():
        put(out.at[0], pair(first))
        put(out.at[1], pair(second))

    if direct:
        order = sorted(
            [(k, i) for k in range(chunks) for i in range(2)], key=lambda ki: ki[0] + LEAD * ki[1]
        )

        def s_copy(k, i):
            return copy(
                nxt.at[k, i], carry.at[:, piece(2 * i + c, k), :],
                s_send.at[k, i], s_recv.at[k, i], {"tm": 2 + c},
            )

        def back_copy(k):
            return copy(
                nxt.at[k, 0], carry.at[:, piece(c, k), :],
                z_send.at[k, 0], e_recv.at[1, k], {"tm": c},
            )

        def relay_copy(k):
            ref = carry.at[:, piece(d, k), :]
            return copy(ref, ref, z_send.at[k, 0], z_recv.at[k], {"win": 1})

        def up_copy(k):
            return copy(
                nxt.at[k, 1], carry.at[:, piece(d, k), :],
                z_send.at[k, 1], z_recv.at[k], {"win": 1},
            )

        @pl.when((z == 0) & (x == 0))
        def _():
            put_split(wsp, pair(chips.at[0]))
            for k, i in order:
                real = identity_rows(2 * i + c, k)
                put(nxt.at[k, i], row_product((real, jnp.zeros_like(real)), wsp))
                s_copy(k, i).start()
            local()
            for k in range(chunks):
                back_copy(k).wait_recv()
                relay_copy(k).start()
            finish_first()
            for k in range(chunks):
                relay_copy(k).wait_send()
            for k in range(chunks):
                for i in range(2):
                    s_copy(k, i).wait_send()

        @pl.when((z == 0) & (x == 1))
        def _():
            put_split(wsp, pair(chips.at[1]))
            for k, i in order:
                s_copy(k, i).wait_recv()
                g_copy(i, c, k).start()
                put(nxt.at[k, i], row_product(pair(carry.at[:, piece(2 * i + c, k), :]), wsp))
                (up_copy if i else back_copy)(k).start()
            local()
            for k in range(chunks):
                for i in range(2):
                    g_copy(i, 1 - c, k).wait_recv()
            finish()
            for k in range(chunks):
                for i in range(2):
                    g_copy(i, c, k).wait_send()
                    (up_copy if i else back_copy)(k).wait_send()
    else:
        @pl.when(z == 0)
        def _():
            exchange()
            whole_window()
            for k in range(chunks):
                real = identity_rows(d, k)
                put(nxt.at[k, 0], row_product((real, jnp.zeros_like(real)), wsp))
                z_copy(k, 1).start()
            chips_before()
            finish_first()
            for k in range(chunks):
                z_copy(k, 1).wait_send()
            exchange_sent()

    @pl.when(z > 0)
    def _():
        exchange()

        @pl.when(z < last)
        def _():
            whole_window()

        @pl.when(z > 1)
        def _():
            chips_before()

        for k in range(chunks):
            ref = carry.at[:, piece(d, k), :]
            z_copy(k, z).wait_recv()
            for j in others:
                e_copy(x, j, k).start()
            g_copy(x, c, k).start()

            @pl.when(z < last)
            def _():
                put(nxt.at[k, 0], row_product(pair(ref), wsp))
                z_copy(k, z + 1).start()

        for k in range(chunks):
            for j in others:
                e_copy(j, x, k).wait_recv()
                g_copy(j, c, k).start()

        @pl.when(z == 1)
        def _():
            chips_before()

        for k in range(chunks):
            g_copy(x, 1 - c, k).wait_recv()
            for j in others:
                g_copy(j, 1 - c, k).wait_recv()
        finish()
        for k in range(chunks):
            for j in others:
                e_copy(x, j, k).wait_send()
                g_copy(j, c, k).wait_send()
            g_copy(x, c, k).wait_send()

        @pl.when(z < last)
        def _():
            for k in range(chunks):
                z_copy(k, z + 1).wait_send()

        exchange_sent()

    t_copy.wait_send()


def on_device(tm, windows, unitaries):
    u = unitaries[0, 0]
    width = u.shape[-1]
    nx = tm // 2
    dma = pltpu.SemaphoreType.DMA
    mat = pltpu.VMEM((2, width, width), F32)
    chunks = carry_chunks(width // tm)
    step = width // tm // chunks
    result = pl.pallas_call(
        functools.partial(kernel, tm, windows),
        out_shape=jax.ShapeDtypeStruct(u.shape, F32),
        in_specs=[pl.BlockSpec(memory_space=pl.ANY)],
        out_specs=pl.BlockSpec(memory_space=pltpu.VMEM),
        scratch_shapes=[
            pltpu.VMEM((2, 2, width, width), F32),
            mat, mat, pltpu.VMEM((nx, 2, width, width), F32), mat, mat, mat, mat,
            pltpu.VMEM((chunks, 2, 2, step, width), F32),
            pltpu.VMEM((4, width, width), BF16),
            dma((2,)), dma, dma,
            dma((nx, PIECES)), dma((nx, PIECES)), dma((nx, PIECES)), dma((nx, PIECES)),
            dma((chunks, 2)), dma((chunks, 2)), dma((chunks, 2)), dma((chunks,)),
            dma((nx, chunks)), dma((nx, chunks)), dma((nx, chunks)), dma((nx, chunks)),
        ],
        compiler_params=pltpu.CompilerParams(
            collective_id=0, has_side_effects=True, vmem_limit_bytes=52 * 1024 * 1024
        ),
    )(u)
    return result[None, None]


def solution(mesh):
    placed = P(("groups", "win"), "tm", None, None, None, None)
    return jax.shard_map(
        functools.partial(on_device, mesh.shape["tm"], mesh.shape["win"]),
        mesh=mesh,
        in_specs=(placed,),
        out_specs=placed,
        check_vma=False,
    )
```

```python
import functools
import jax
import jax.numpy as jnp
from jax import lax
from jax.sharding import PartitionSpec as P
from jax.experimental import pallas as pl
from jax.experimental.pallas import tpu as pltpu

F32 = jnp.float32
BF16 = jnp.bfloat16
MESH = pl.DeviceIdType.MESH
MOST_CHUNKS = 4
LEAD = 4
PIECES = 2
NT = (((1,), (1,)), ((), ()))
NN = (((1,), (0,)), ((), ()))


def split(a):
    hi = a.astype(BF16)
    return hi, (a - hi.astype(F32)).astype(BF16)


def real_dot(a, b, dims):
    def dot(p, q):
        return lax.dot_general(p, q, dims, preferred_element_type=F32)

    return dot(a[0], b[0]) + (dot(a[0], b[1]) + dot(a[1], b[0]))


def product(a, b, transposed=False):
    dims = NT if transposed else NN
    ar, ai = split(a[0]), split(a[1])
    br, bi = split(b[0]), split(b[1])
    real = real_dot(ar, br, dims) - real_dot(ai, bi, dims)
    imag = real_dot(ar, bi, dims) + real_dot(ai, br, dims)
    return real, imag


def put_split(ref, value):
    ref[0], ref[1] = split(value[0])
    ref[2], ref[3] = split(value[1])


def row_product(a, w):
    m = a[0].shape[0]
    (rh, rl), (ih, il) = split(a[0]), split(a[1])
    stack = jnp.concatenate([rh, ih, rl, il], axis=0)
    top = jnp.concatenate([rh, ih], axis=0)

    def dot(p, q):
        return lax.dot_general(p, q, NT, preferred_element_type=F32)

    by_real = dot(stack, w[0])
    by_real = by_real[: 2 * m] + by_real[2 * m :] + dot(top, w[1])
    by_imag = dot(stack, w[2])
    by_imag = by_imag[: 2 * m] + by_imag[2 * m :] + dot(top, w[3])
    return by_real[:m] - by_imag[m:], by_real[m:] + by_imag[:m]


def pair(ref):
    return ref[0], ref[1]


def put(ref, value):
    ref[0] = value[0]
    ref[1] = value[1]


def carry_chunks(rows):
    return max(1, min(MOST_CHUNKS, rows // 8))


def kernel(
    tm, windows, u_hbm, out,
    u, total, sib, chips, win, first, second, carry, nxt, wsp,
    u_sem, t_send, t_recv, c_send, c_recv, f_send, f_recv,
    s_send, s_recv, z_send, z_recv, e_send, e_recv, g_send, g_recv,
):
    d = lax.axis_index("tm")
    z = lax.axis_index("win")
    x, c = d // 2, d % 2
    nx = tm // 2
    direct = nx == 2
    width = u.shape[-1]
    half = width // 2
    rows = width // tm
    chunks = carry_chunks(rows)
    step = rows // chunks
    part = half // PIECES
    mate = {"tm": x * 2 + (1 - c)}
    last = windows - 1

    loads = [pltpu.make_async_copy(u_hbm.at[s], u.at[s], u_sem.at[s]) for s in range(2)]
    for load in loads:
        load.start()

    barrier = pltpu.get_barrier_semaphore()

    def greet(to):
        pl.semaphore_signal(barrier, inc=1, device_id=to, device_id_type=MESH)

    greet(mate)
    for o in range(1, nx):
        greet({"tm": ((x + o) % nx) * 2 + c})
        greet({"tm": ((x + o) % nx) * 2 + (1 - c)})

    @pl.when(z > 0)
    def _():
        greet({"win": z - 1})

    @pl.when(z < last)
    def _():
        greet({"win": z + 1})

    for load in loads:
        load.wait()
    put(total, product(pair(u.at[1]), pair(u.at[0])))

    inner = (z > 0) & (z < last)
    @pl.when(inner)
    def _():
        pl.semaphore_wait(barrier, 2 * nx + 1)

    @pl.when(jnp.logical_not(inner))
    def _():
        pl.semaphore_wait(barrier, 2 * nx)

    def copy(src, dst, send, recv, to):
        return pltpu.make_async_remote_copy(
            src_ref=src, dst_ref=dst, send_sem=send, recv_sem=recv,
            device_id=to, device_id_type=MESH,
        )

    t_copy = copy(total, sib, t_send, t_recv, mate)
    t_copy.start()
    t_copy.wait_recv()

    @pl.when(c == 0)
    def _():
        put(chips.at[x], product(pair(sib), pair(total)))

    @pl.when(c == 1)
    def _():
        put(chips.at[x], product(pair(total), pair(sib)))

    others = [(x + o) % nx for o in range(1, nx)]

    def local():
        @pl.when(c == 0)
        def _():
            put(first, pair(u.at[0]))
            put(second, pair(total))

        @pl.when(c == 1)
        def _():
            put(first, product(pair(u.at[0]), pair(sib)))
            put(second, pair(chips.at[x]))

    def band(core, q):
        return pl.ds(pl.multiple_of(core * half + q * part, part), part)

    def c_copy(j, to, q):
        ref = chips.at[j, :, band(c, q), :]
        return copy(ref, ref, c_send.at[to, q], c_recv.at[j, q], {"tm": to * 2 + c})

    def f_copy(j, core, q):
        ref = chips.at[j, :, band(core, q), :]
        return copy(ref, ref, f_send.at[j, q], f_recv.at[j, q], mate)

    def exchange():
        for q in range(PIECES):
            for j in others:
                c_copy(x, j, q).start()
        local()
        for q in range(PIECES):
            for j in others:
                c_copy(j, x, q).wait_recv()
                f_copy(j, c, q).start()
        for q in range(PIECES):
            for j in others:
                f_copy(j, 1 - c, q).wait_recv()

    def exchange_sent():
        for q in range(PIECES):
            for j in others:
                c_copy(x, j, q).wait_send()
                f_copy(j, c, q).wait_send()

    def apply_before(before):
        put(first, product(pair(first), before))
        put(second, product(pair(second), before))

    def whole_window():
        if direct:
            put(win, product(pair(chips.at[1]), pair(chips.at[0])))
        else:
            put(win, pair(chips.at[0]))

            def join(j, _):
                put(win, product(pair(chips.at[j]), pair(win)))
                return 0

            lax.fori_loop(1, nx, join, 0)
        put_split(wsp, pair(win))

    def chips_before():
        @pl.when(x > 0)
        def _():
            if not direct:
                put(win, pair(chips.at[0]))

                def join(j, _):
                    put(win, product(pair(chips.at[j]), pair(win)))
                    return 0

                lax.fori_loop(1, x, join, 0)
                apply_before(pair(win))
            else:
                apply_before(pair(chips.at[0]))

    def piece(owner, k):
        return pl.ds(pl.multiple_of(owner * rows + k * step, step), step)

    def identity_rows(owner, k):
        row = lax.broadcasted_iota(jnp.int32, (step, width), 0) + (owner * rows + k * step)
        column = lax.broadcasted_iota(jnp.int32, (step, width), 1)
        return (row == column).astype(F32)

    def z_copy(k, to):
        return copy(
            nxt.at[k, 0], carry.at[:, piece(d, k), :],
            z_send.at[k, 0], z_recv.at[k], {"win": to},
        )

    def e_copy(j, to, k):
        ref = carry.at[:, piece(j * 2 + c, k), :]
        return copy(ref, ref, e_send.at[to, k], e_recv.at[j, k], {"tm": to * 2 + c})

    def g_copy(j, core, k):
        ref = carry.at[:, piece(j * 2 + core, k), :]
        return copy(ref, ref, g_send.at[j, k], g_recv.at[j, k], mate)

    def both_copy(to, k):
        ref = carry.at[:, piece(d, k), :]
        return copy(ref, ref, g_send.at[to, k], g_recv.at[x, k], {"tm": to * 2 + (1 - c)})

    def finish():
        before = pair(carry)
        put(out.at[0], product(pair(first), before, transposed=True))
        put(out.at[1], product(pair(second), before, transposed=True))

    def finish_first():
        put(out.at[0], pair(first))
        put(out.at[1], pair(second))

    if direct:
        order = sorted(
            [(k, i) for k in range(chunks) for i in range(2)], key=lambda ki: ki[0] + LEAD * ki[1]
        )

        def s_copy(k, i):
            return copy(
                nxt.at[k, i], carry.at[:, piece(2 * i + c, k), :],
                s_send.at[k, i], s_recv.at[k, i], {"tm": 2 + c},
            )

        def back_copy(k):
            return copy(
                nxt.at[k, 0], carry.at[:, piece(c, k), :],
                z_send.at[k, 0], e_recv.at[1, k], {"tm": c},
            )

        def relay_copy(k):
            ref = carry.at[:, piece(d, k), :]
            return copy(ref, ref, z_send.at[k, 0], z_recv.at[k], {"win": 1})

        def up_copy(k):
            return copy(
                nxt.at[k, 1], carry.at[:, piece(d, k), :],
                z_send.at[k, 1], z_recv.at[k], {"win": 1},
            )

        @pl.when((z == 0) & (x == 0))
        def _():
            put_split(wsp, pair(chips.at[0]))
            for k, i in order:
                real = identity_rows(2 * i + c, k)
                put(nxt.at[k, i], row_product((real, jnp.zeros_like(real)), wsp))
                s_copy(k, i).start()
            local()
            for k in range(chunks):
                back_copy(k).wait_recv()
                relay_copy(k).start()
            finish_first()
            for k in range(chunks):
                relay_copy(k).wait_send()
            for k in range(chunks):
                for i in range(2):
                    s_copy(k, i).wait_send()

        @pl.when((z == 0) & (x == 1))
        def _():
            put_split(wsp, pair(chips.at[1]))
            for k, i in order:
                s_copy(k, i).wait_recv()
                g_copy(i, c, k).start()
                put(nxt.at[k, i], row_product(pair(carry.at[:, piece(2 * i + c, k), :]), wsp))
                (up_copy if i else back_copy)(k).start()
            local()
            for k in range(chunks):
                for i in range(2):
                    g_copy(i, 1 - c, k).wait_recv()
            finish()
            for k in range(chunks):
                for i in range(2):
                    g_copy(i, c, k).wait_send()
                    (up_copy if i else back_copy)(k).wait_send()
    else:
        @pl.when(z == 0)
        def _():
            exchange()
            whole_window()
            for k in range(chunks):
                real = identity_rows(d, k)
                put(nxt.at[k, 0], row_product((real, jnp.zeros_like(real)), wsp))
                z_copy(k, 1).start()
            chips_before()
            finish_first()
            for k in range(chunks):
                z_copy(k, 1).wait_send()
            exchange_sent()

    @pl.when(z > 0)
    def _():
        exchange()

        @pl.when(z < last)
        def _():
            whole_window()

        @pl.when(z > 1)
        def _():
            chips_before()

        for k in range(chunks):
            ref = carry.at[:, piece(d, k), :]
            z_copy(k, z).wait_recv()
            for j in others:
                e_copy(x, j, k).start()
                if k == chunks - 1:
                    both_copy(j, k).start()
            g_copy(x, c, k).start()

            @pl.when(z < last)
            def _():
                put(nxt.at[k, 0], row_product(pair(ref), wsp))
                z_copy(k, z + 1).start()

        for k in range(chunks):
            for j in others:
                e_copy(j, x, k).wait_recv()
                if k < chunks - 1:
                    g_copy(j, c, k).start()

        @pl.when(z == 1)
        def _():
            chips_before()

        for k in range(chunks):
            g_copy(x, 1 - c, k).wait_recv()
            for j in others:
                g_copy(j, 1 - c, k).wait_recv()
        finish()
        for k in range(chunks):
            for j in others:
                e_copy(x, j, k).wait_send()
                (g_copy(j, c, k) if k < chunks - 1 else both_copy(j, k)).wait_send()
            g_copy(x, c, k).wait_send()

        @pl.when(z < last)
        def _():
            for k in range(chunks):
                z_copy(k, z + 1).wait_send()

        exchange_sent()

    t_copy.wait_send()


def on_device(tm, windows, unitaries):
    u = unitaries[0, 0]
    width = u.shape[-1]
    nx = tm // 2
    dma = pltpu.SemaphoreType.DMA
    mat = pltpu.VMEM((2, width, width), F32)
    chunks = carry_chunks(width // tm)
    step = width // tm // chunks
    result = pl.pallas_call(
        functools.partial(kernel, tm, windows),
        out_shape=jax.ShapeDtypeStruct(u.shape, F32),
        in_specs=[pl.BlockSpec(memory_space=pl.ANY)],
        out_specs=pl.BlockSpec(memory_space=pltpu.VMEM),
        scratch_shapes=[
            pltpu.VMEM((2, 2, width, width), F32),
            mat, mat, pltpu.VMEM((nx, 2, width, width), F32), mat, mat, mat, mat,
            pltpu.VMEM((chunks, 2, 2, step, width), F32),
            pltpu.VMEM((4, width, width), BF16),
            dma((2,)), dma, dma,
            dma((nx, PIECES)), dma((nx, PIECES)), dma((nx, PIECES)), dma((nx, PIECES)),
            dma((chunks, 2)), dma((chunks, 2)), dma((chunks, 2)), dma((chunks,)),
            dma((nx, chunks)), dma((nx, chunks)), dma((nx, chunks)), dma((nx, chunks)),
        ],
        compiler_params=pltpu.CompilerParams(
            collective_id=0, has_side_effects=True, vmem_limit_bytes=52 * 1024 * 1024
        ),
    )(u)
    return result[None, None]


def solution(mesh):
    placed = P(("groups", "win"), "tm", None, None, None, None)
    return jax.shard_map(
        functools.partial(on_device, mesh.shape["tm"], mesh.shape["win"]),
        mesh=mesh,
        in_specs=(placed,),
        out_specs=placed,
        check_vma=False,
    )
```
